32 devices in a mesh: row: 16 (over z, x, core), col: 2 (over y).
Axes of the slice: x: 2, y: 2, z: 4, core: 2. Of those that a mesh axis runs over, the one named last changes fastest.
Arguments:
- tiles: bfloat16 [16, 2, 256, 128, 128], P('row', 'col'), may hold values from 0 to 0.00064849854
- tile_row: int32 [16, 2, 256], P('row', 'col'), may hold values from 0 to 16, as said below
- tile_col: int32 [16, 2, 256], P('row', 'col'), may hold values from 0 to 128, as said below
- right_vecs: bfloat16 [256, 32, 128], P(('row', 'col')), may hold values from -6 to 6
- left_vecs: bfloat16 [256, 32, 128], P(('row', 'col')), may hold values from -6 to 6
Outputs:
- right_next: float32 [256, 32, 128], P(('row', 'col'))
- left_next: float32 [256, 32, 128], P(('row', 'col'))
- gram: float32 [32, 32], replicated
The draws below stay inside these ranges and needn't reach their ends.
Inputs may be any that keep to these rules, and one draw needn't show every extreme that they name: Value 16 marks an empty slot; a slot is empty in tile_row exactly when it is empty in tile_col; live slots come first on each device; each device has 128 to 256 live slots and some device has all 256 live. `tile_col`: value 128 marks an empty slot, in the same slots as tile_row.
All inputs are finite; a program needn't handle non-finite values.
Results may differ from the reference program's by a relative error of at most 0.0003.
Values may be sent and summed in bfloat16 or wider, within the bound.
A program may use at most 64 MiB of HBM per device.

```python
import jax
import jax.numpy as jnp
from jax import lax

TILE = 128
K = 32
TRP = 8
RT = 16
CT = 128
NT = 256
NB = 32768
TMAX = 256
N_ROW = 16
N_COL = 2


def slot_pattern(key):
    base = jax.random.fold_in(key, 7)
    key_count, key_rows, key_cols, key_full = jax.random.split(base, 4)
    device_count = N_ROW * N_COL
    counts = TMAX // 2 + jax.random.randint(key_count, (device_count,), 0, TMAX // 2 + 1)
    full_device = jax.random.randint(key_full, (), 0, device_count)
    counts = jnp.where(jnp.arange(device_count) == full_device, TMAX, counts)
    live = jnp.arange(TMAX)[None, :] < counts[:, None]
    slot_rows = jax.random.randint(key_rows, (device_count, TMAX), 0, RT)
    slot_cols = jax.random.randint(key_cols, (device_count, TMAX), 0, CT)
    slot_rows = jnp.where(live, slot_rows, RT).reshape(N_ROW, N_COL, TMAX)
    slot_cols = jnp.where(live, slot_cols, CT).reshape(N_ROW, N_COL, TMAX)
    return (slot_rows.astype(jnp.int32), slot_cols.astype(jnp.int32))


def draw_tile_row(key, part):
    return slot_pattern(key)[0]


def draw_tile_col(key, part):
    return slot_pattern(key)[1]


def levels(stream_key, shape, pieces, least, top_value):
    factor_of = 1.0
    for axis_at, parts in pieces:
        heights = jax.random.uniform(jax.random.fold_in(jax.random.fold_in(stream_key, 6), axis_at), (parts,), jnp.float32, least / len(pieces), top_value / len(pieces))
        factor_of = factor_of * jnp.repeat(jnp.exp(heights), shape[axis_at] // parts).reshape((-1,) + (1,) * (len(shape) - 1 - axis_at))
    return factor_of


def gaussian(stream_key, shape, width, bound, pieces=(), held_as=jnp.bfloat16):
    result = width * jax.random.normal(stream_key, shape, jnp.float32)
    if pieces:
        result = result * levels(stream_key, shape, pieces, -0.22, 0.18)
    return jnp.clip(result, -bound, bound).astype(held_as)


def setup_inputs(seed: int = 0) -> dict:
    key_list = jax.random.split(jax.random.key(seed), 6)
    tiles = jnp.clip(0.00064849854 * jax.random.uniform(key_list[0], (N_ROW, N_COL, TMAX, TILE, TILE), jnp.float32) ** levels(key_list[0], (N_ROW, N_COL, TMAX, TILE, TILE), ((0, 16), (1, 2)), -0.2, 0.2), 0.0, 0.00064849854).astype(jnp.bfloat16)
    tile_row = draw_tile_row(jax.random.fold_in(key_list[5], 71), 0)
    tile_col = draw_tile_col(jax.random.fold_in(key_list[5], 71), 0)
    right_vecs = gaussian(key_list[3], (NT, K, TILE), 1.0, 6.0, ((0, 32),))
    left_vecs = gaussian(key_list[4], (NT, K, TILE), 1.0, 6.0, ((0, 32),))
    return dict(tiles=tiles, tile_row=tile_row, tile_col=tile_col, right_vecs=right_vecs, left_vecs=left_vecs)


def reference(tiles, tile_row, tile_col, right_vecs, left_vecs):
    highest = lax.Precision.HIGHEST
    row_block = jnp.arange(N_ROW, dtype=jnp.int32)[:, None, None]
    col_block = jnp.arange(N_COL, dtype=jnp.int32)[None, :, None]
    live = tile_row < RT
    global_rows = jnp.where(live, row_block * RT + tile_row, NT).astype(jnp.int32)
    global_cols = jnp.where(live, ((tile_col // TRP) * N_COL + col_block) * TRP + tile_col % TRP, NT).astype(jnp.int32)
    flat_tiles = tiles.reshape(N_ROW * N_COL, TMAX, TILE, TILE)
    flat_rows = global_rows.reshape(N_ROW * N_COL, TMAX)
    flat_cols = global_cols.reshape(N_ROW * N_COL, TMAX)
    right_float = right_vecs.astype(jnp.float32)
    left_float = left_vecs.astype(jnp.float32)

    def device_step(carry, item):
        image_right, image_left = carry
        tile_block, row_index, col_index = item
        tile_float = tile_block.astype(jnp.float32)
        right_in = jnp.take(right_float, jnp.minimum(col_index, NT - 1), axis=0)
        left_in = jnp.take(left_float, jnp.minimum(row_index, NT - 1), axis=0)
        forward = jnp.einsum("sef,skf->ske", tile_float, right_in, precision=highest)
        backward = jnp.einsum("sef,ske->skf", tile_float, left_in, precision=highest)
        image_right = image_right.at[row_index].add(forward, mode="drop")
        image_left = image_left.at[col_index].add(backward, mode="drop")
        return (image_right, image_left), None

    start = (jnp.zeros((NT, K, TILE), jnp.float32), jnp.zeros((NT, K, TILE), jnp.float32))
    (image_right, image_left), _ = lax.scan(device_step, start, (flat_tiles, flat_rows, flat_cols))
    gram = jnp.einsum("tke,tle->kl", left_float, image_right, precision=highest) * (NB ** -0.5)
    right_next = image_right - jnp.einsum("tke,kl->tle", right_float, gram, precision=highest)
    left_next = image_left - jnp.einsum("tle,kl->tke", left_float, gram, precision=highest)
    return right_next, left_next, gram
```

```python
import functools

import jax
import jax.numpy as jnp
from jax import lax
from jax.experimental import pallas as pl
from jax.experimental.pallas import tpu as pltpu
from jax.sharding import PartitionSpec as P

MESH = pl.DeviceIdType.MESH
F32 = jnp.float32
BF16 = jnp.bfloat16
GROUP = 8


def split(value):
    high = value.astype(BF16)
    low = (value - high.astype(F32)).astype(BF16)
    return high, low


def mul(a, b, dims=(((1,), (0,)), ((), ()))):
    return lax.dot_general(a, b, dims, preferred_element_type=F32)


def kernel(
    sizes,
    row_s,
    col_s,
    row_v,
    col_v,
    right,
    left,
    tiles,
    out_r,
    out_l,
    out_g,
    tbuf,
    cv,
    rv,
    prod,
    zp,
    zc,
    zs,
    zx,
    zz,
    yp,
    yl,
    gz,
    gx,
    gc,
    gy,
    tile_sem,
    send_sem,
    left_sem,
    right_sem,
    zc_sem,
    zx_sem,
    zz_sem,
    y_sem,
    g_sem,
):
    n_r, n_c, outer, inner, chunks = sizes
    piece, vecs, side = right.shape
    slots = tbuf.shape[0]
    step = slots // chunks
    block_rows = piece * n_c
    block_cols = piece * n_r
    part = piece * vecs
    r = lax.axis_index("row")
    c = lax.axis_index("col")
    core = r % 2
    i = (r // 2) % inner
    o = r // (2 * inner)

    def row_of(oo, ii, cc):
        return (oo * inner + ii) * 2 + cc

    partner = (row_of(o, i, 1 - core), c)
    z_far = [(o + d) % outer for d in range(1, outer)]
    z_src = [(o - d + outer) % outer for d in range(1, outer)]
    x_far = [(i + d) % inner for d in range(1, inner)]
    x_src = [(i - d + inner) % inner for d in range(1, inner)]
    y_far = [(c + d) % n_c for d in range(1, n_c)]
    y_src = [(c - d + n_c) % n_c for d in range(1, n_c)]

    def tile_copy(ch):
        at = pl.ds(ch * step, step)
        return pltpu.make_async_copy(tiles.at[0, 0, at], tbuf.at[at], tile_sem.at[ch])

    for ch in range(chunks):
        tile_copy(ch).start()

    barrier = pltpu.get_barrier_semaphore()
    peers = (
        [(row_of(z, i, core), c) for z in z_far]
        + [(row_of(o, x, core), c) for x in x_far]
        + [partner]
        + [(r, y) for y in y_far]
    )
    for peer in peers:
        pl.semaphore_signal(barrier, inc=1, device_id=peer, device_id_type=MESH)
    pl.semaphore_wait(barrier, len(peers))

    sent = []

    def send(src, dst, sem, peer):
        copy = pltpu.make_async_remote_copy(
            src_ref=src,
            dst_ref=dst,
            send_sem=send_sem.at[len(sent)],
            recv_sem=sem,
            device_id=peer,
            device_id_type=MESH,
        )
        copy.start()
        sent.append(copy)

    def landed(ref, sem):
        pltpu.make_async_remote_copy(
            src_ref=ref,
            dst_ref=ref,
            send_sem=send_sem.at[0],
            recv_sem=sem,
            device_id=partner,
            device_id_type=MESH,
        ).wait_recv()

    def cv_at(rr):
        return cv.at[pl.ds(rr * piece, piece)]

    def rv_at(cc):
        return rv.at[pl.ds(cc * piece, piece)]

    for y in y_far:
        send(left, rv_at(c), left_sem.at[c], (r, y))
    for z in z_far:
        send(right, cv_at(r), right_sem.at[r], (row_of(z, i, core), c))
    for x in x_far:
        send(right, cv_at(r), right_sem.at[r], (row_of(o, x, core), c))
    send(right, cv_at(r), right_sem.at[r], partner)
    cv[pl.ds(r * piece, piece)] = right[...]
    rv[pl.ds(c * piece, piece)] = left[...]

    def relay_z():
        for z in z_src:
            got = row_of(z, i, core)
            landed(cv_at(got), right_sem.at[got])
            for x in x_far:
                send(cv_at(got), cv_at(got), right_sem.at[got], (row_of(o, x, core), c))
            send(cv_at(got), cv_at(got), right_sem.at[got], partner)

    def relay_x():
        for z in [o] + z_src:
            for x in x_src:
                got = row_of(z, x, core)
                landed(cv_at(got), right_sem.at[got])
                send(cv_at(got), cv_at(got), right_sem.at[got], partner)

    def take_core():
        for z in [o] + z_src:
            for x in [i] + x_src:
                got = row_of(z, x, 1 - core)
                landed(cv_at(got), right_sem.at[got])

    def images(ch, vec_ref, index, limit, dims):
        def body(g, carry):
            for u in range(GROUP):
                s = ch * step + g * GROUP + u
                x = vec_ref[jnp.minimum(index[s], limit - 1)]
                prod[pl.ds(pl.multiple_of(s * vecs, vecs), vecs), :] = mul(x, tbuf[s], dims)
            return carry

        lax.fori_loop(0, step // GROUP, body, 0)

    plain = (((1,), (0,)), ((), ()))
    across = (((1,), (1,)), ((), ()))

    def gather_sums(index_v, rows, target):
        pick = lax.broadcasted_iota(jnp.int32, (rows, slots), 0) == index_v[...]
        pick = jnp.where(pick, 1.0, 0.0).astype(BF16)

        def body(k, carry):
            high, low = split(prod[pl.ds(k, slots, stride=vecs), :])
            target[pl.ds(k, rows, stride=vecs), :] = mul(pick, high) + mul(pick, low)
            return carry

        lax.fori_loop(0, vecs, body, 0)

    for y in y_src:
        landed(rv_at(y), left_sem.at[y])
    for ch in range(chunks):
        tile_copy(ch).wait()
        images(ch, rv, row_s, block_rows, plain)
        if ch == chunks // 2:
            relay_z()
    relay_x()
    gather_sums(col_v, block_cols, zp)

    z_order = list(zip(z_far, range(1, outer))) + [(o, 0)]
    x_order = list(zip(x_far, range(1, inner))) + [(i, 0)]
    for z, _ in z_order:
        for x, _ in x_order:
            at = pl.ds(row_of(z, x, 1 - core) * part, part)
            slot = z * inner + x
            send(zp.at[at], zc.at[slot], zc_sem.at[slot], partner)
    take_core()
    for ch in range(chunks // 2):
        images(ch, cv, col_s, block_cols, across)
    for z, _ in z_order:
        for x, dx in x_order:
            slot = z * inner + x
            landed(zc.at[slot], zc_sem.at[slot])
            at = pl.ds(row_of(z, x, core) * part, part)
            zs[slot] = zp[at] + zc[slot]
            if dx:
                send(zs.at[slot], zx.at[dx - 1, z], zx_sem.at[dx - 1, z], (row_of(o, x, core), c))
    for ch in range(chunks // 2, chunks):
        images(ch, cv, col_s, block_cols, across)
    gather_sums(row_v, block_rows, yp)
    for y in y_far:
        dy = (y - c + n_c) % n_c
        send(yp.at[pl.ds(y * part, part)], yl.at[dy], y_sem.at[dy], (r, y))

    def gram_step(a, total):
        at = pl.ds(pl.multiple_of(a * vecs, vecs), vecs)
        high, low = split(yp[at, :])
        mine = rv[a]
        return total + mul(mine, high, across) + mul(mine, low, across)

    gram = lax.fori_loop(0, block_rows, gram_step, jnp.zeros((vecs, vecs), F32))
    used = 0

    def spread(value, buf, me, far, src, peer):
        nonlocal used
        buf[me] = value
        for f in far:
            send(buf.at[me], buf.at[me], g_sem.at[used + me], peer(f))
        for s in src:
            landed(buf.at[s], g_sem.at[used + s])
        used += buf.shape[0]
        total = buf[0]
        for q in range(1, buf.shape[0]):
            total = total + buf[q]
        return total

    gram = spread(gram, gc, core, [1 - core], [1 - core], lambda f: (row_of(o, i, f), c))
    gram = spread(gram, gx, i, x_far, x_src, lambda f: (row_of(o, f, core), c))

    for z, dz in z_order:
        slot = z * inner + i
        total = zs[slot]
        for d in range(1, inner):
            landed(zx.at[d - 1, z], zx_sem.at[d - 1, z])
            total = total + zx[d - 1, z]
        zs[slot] = total
        if dz:
            send(zs.at[slot], zz.at[dz - 1], zz_sem.at[dz - 1], (row_of(z, i, core), c))

    gram = spread(gram, gy, c, y_far, y_src, lambda f: (r, f))
    gram = spread(gram, gz, o, z_far, z_src, lambda f: (row_of(f, i, core), c))
    gram = gram * (block_cols * n_c * side) ** (-0.5)
    out_g[...] = gram
    high, low = split(gram)
    turned = gram.T
    turned_high, turned_low = split(turned)

    y_total = yp[pl.ds(c * part, part), :]
    for d in range(1, n_c):
        landed(yl.at[d], y_sem.at[d])
        y_total = y_total + yl[d]
    for t in range(piece):
        at = slice(t * vecs, (t + 1) * vecs)
        out_r[t] = y_total[at] - (mul(turned_high, right[t]) + mul(turned_low, right[t]))
    z_total = zs[o * inner + i]
    for d in range(1, outer):
        landed(zz.at[d - 1], zz_sem.at[d - 1])
        z_total = z_total + zz[d - 1]
    for t in range(piece):
        at = slice(t * vecs, (t + 1) * vecs)
        out_l[t] = z_total[at] - (mul(high, left[t]) + mul(low, left[t]))
    for copy in sent:
        copy.wait_send()


def solution(mesh):
    n_r, n_c = mesh.shape["row"], mesh.shape["col"]
    half = n_r // 2
    inner = 1 << ((half.bit_length() - 1) // 2)
    outer = half // inner

    def per_device(tiles, tile_row, tile_col, right_vecs, left_vecs):
        slots, side = tiles.shape[2], tiles.shape[3]
        piece, vecs, _ = right_vecs.shape
        chunks = 8
        part = piece * vecs
        block_rows, block_cols = piece * n_c, piece * n_r
        planes = outer * inner
        sends = (
            2 * (n_c - 1)
            + (outer - 1)
            + (inner - 1)
            + 1
            + (outer - 1) * inner
            + outer * (inner - 1)
            + planes
            + outer * (inner - 1)
            + (outer - 1)
            + 1
            + (inner - 1)
            + (n_c - 1)
            + (outer - 1)
        )
        vmem = pl.BlockSpec(memory_space=pltpu.VMEM)
        smem = pl.BlockSpec(memory_space=pltpu.SMEM)
        dma = pltpu.SemaphoreType.DMA
        row_s = tile_row.reshape(slots)
        col_s = tile_col.reshape(slots)
        return pl.pallas_call(
            functools.partial(kernel, (n_r, n_c, outer, inner, chunks)),
            out_shape=(
                jax.ShapeDtypeStruct((piece, vecs, side), F32),
                jax.ShapeDtypeStruct((piece, vecs, side), F32),
                jax.ShapeDtypeStruct((vecs, vecs), F32),
            ),
            in_specs=[smem, smem, vmem, vmem, vmem, vmem, pl.BlockSpec(memory_space=pl.ANY)],
            out_specs=(vmem, vmem, vmem),
            scratch_shapes=[
                pltpu.VMEM((slots, side, side), BF16),
                pltpu.VMEM((block_cols, vecs, side), BF16),
                pltpu.VMEM((block_rows, vecs, side), BF16),
                pltpu.VMEM((slots * vecs, side), F32),
                pltpu.VMEM((block_cols * vecs, side), F32),
                pltpu.VMEM((planes, part, side), F32),
                pltpu.VMEM((planes, part, side), F32),
                pltpu.VMEM((max(inner - 1, 1), outer, part, side), F32),
                pltpu.VMEM((max(outer - 1, 1), part, side), F32),
                pltpu.VMEM((block_rows * vecs, side), F32),
                pltpu.VMEM((n_c, part, side), F32),
                pltpu.VMEM((outer, vecs, vecs), F32),
                pltpu.VMEM((inner, vecs, vecs), F32),
                pltpu.VMEM((2, vecs, vecs), F32),
                pltpu.VMEM((n_c, vecs, vecs), F32),
                dma((chunks,)),
                dma((sends,)),
                dma((n_c,)),
                dma((n_r,)),
                dma((planes,)),
                dma((max(inner - 1, 1), outer)),
                dma((max(outer - 1, 1),)),
                dma((n_c,)),
                dma((outer + inner + 2 + n_c,)),
            ],
            compiler_params=pltpu.CompilerParams(
                collective_id=0, has_side_effects=True, vmem_limit_bytes=60 * 1024 * 1024
            ),
            name="arnoldi_step",
        )(row_s, col_s, row_s.reshape(1, slots), col_s.reshape(1, slots), right_vecs, left_vecs, tiles)

    placed = (
        P("row", "col", None, None, None),
        P("row", "col", None),
        P("row", "col", None),
        P(("row", "col"), None, None),
        P(("row", "col"), None, None),
    )
    return jax.shard_map(
        per_device,
        mesh=mesh,
        in_specs=placed,
        out_specs=(P(("row", "col"), None, None), P(("row", "col"), None, None), P()),
        check_vma=False,
    )
```

```python
import functools

import jax
import jax.numpy as jnp
from jax import lax
from jax.experimental import pallas as pl
from jax.experimental.pallas import tpu as pltpu
from jax.sharding import PartitionSpec as P

MESH = pl.DeviceIdType.MESH
F32 = jnp.float32
BF16 = jnp.bfloat16
GROUP = 8
PAD = 1


def split(value):
    high = value.astype(BF16)
    low = (value - high.astype(F32)).astype(BF16)
    return high, low


def mul(a, b, dims=(((1,), (0,)), ((), ()))):
    return lax.dot_general(a, b, dims, preferred_element_type=F32)


def kernel(
    sizes,
    row_s,
    col_s,
    row_v,
    col_v,
    right,
    left,
    tiles,
    out_y,
    out_z,
    out_g,
    tbuf,
    cv,
    rv,
    prod,
    zp,
    zc,
    zs,
    zx,
    zz,
    yp,
    yl,
    gz,
    gx,
    gc,
    gy,
    tile_sem,
    send_sem,
    left_sem,
    right_sem,
    zc_sem,
    zx_sem,
    zz_sem,
    y_sem,
    g_sem,
):
    n_r, n_c, outer, inner, chunks = sizes
    piece, vecs, side = right.shape
    slots = tbuf.shape[0]
    step = slots // chunks
    block_rows = piece * n_c
    block_cols = piece * n_r
    wide = vecs + PAD
    part = piece * wide
    r = lax.axis_index("row")
    c = lax.axis_index("col")
    core = r % 2
    i = (r // 2) % inner
    o = r // (2 * inner)

    def row_of(oo, ii, cc):
        return (oo * inner + ii) * 2 + cc

    partner = (row_of(o, i, 1 - core), c)
    z_far = [(o + d) % outer for d in range(1, outer)]
    z_src = [(o - d + outer) % outer for d in range(1, outer)]
    x_far = [(i + d) % inner for d in range(1, inner)]
    x_src = [(i - d + inner) % inner for d in range(1, inner)]
    y_far = [(c + d) % n_c for d in range(1, n_c)]
    y_src = [(c - d + n_c) % n_c for d in range(1, n_c)]

    def tile_copy(ch):
        at = pl.ds(ch * step, step)
        return pltpu.make_async_copy(tiles.at[0, 0, at], tbuf.at[at], tile_sem.at[ch])

    for ch in range(chunks):
        tile_copy(ch).start()

    barrier = pltpu.get_barrier_semaphore()
    peers = (
        [(row_of(z, i, core), c) for z in z_far]
        + [(row_of(o, x, core), c) for x in x_far]
        + [partner]
        + [(r, y) for y in y_far]
    )
    for peer in peers:
        pl.semaphore_signal(barrier, inc=1, device_id=peer, device_id_type=MESH)
    pl.semaphore_wait(barrier, len(peers))

    sent = []

    def send(src, dst, sem, peer):
        copy = pltpu.make_async_remote_copy(
            src_ref=src,
            dst_ref=dst,
            send_sem=send_sem.at[len(sent)],
            recv_sem=sem,
            device_id=peer,
            device_id_type=MESH,
        )
        copy.start()
        sent.append(copy)

    def landed(ref, sem):
        pltpu.make_async_remote_copy(
            src_ref=ref,
            dst_ref=ref,
            send_sem=send_sem.at[0],
            recv_sem=sem,
            device_id=partner,
            device_id_type=MESH,
        ).wait_recv()

    def cv_at(rr):
        return cv.at[pl.ds(rr * piece, piece)]

    def rv_at(cc):
        return rv.at[pl.ds(cc * piece, piece)]

    for y in y_far:
        send(left, rv_at(c), left_sem.at[c], (r, y))
    for z in z_far:
        send(right, cv_at(r), right_sem.at[r], (row_of(z, i, core), c))
    for x in x_far:
        send(right, cv_at(r), right_sem.at[r], (row_of(o, x, core), c))
    send(right, cv_at(r), right_sem.at[r], partner)
    cv[pl.ds(r * piece, piece)] = right[...]
    rv[pl.ds(c * piece, piece)] = left[...]

    def relay_z():
        for z in z_src:
            got = row_of(z, i, core)
            landed(cv_at(got), right_sem.at[got])
            for x in x_far:
                send(cv_at(got), cv_at(got), right_sem.at[got], (row_of(o, x, core), c))
            send(cv_at(got), cv_at(got), right_sem.at[got], partner)

    def relay_x():
        for z in [o] + z_src:
            for x in x_src:
                got = row_of(z, x, core)
                landed(cv_at(got), right_sem.at[got])
                send(cv_at(got), cv_at(got), right_sem.at[got], partner)

    def take_core():
        for z in [o] + z_src:
            for x in [i] + x_src:
                got = row_of(z, x, 1 - core)
                landed(cv_at(got), right_sem.at[got])

    def images(ch, vec_ref, index, limit, dims):
        def body(g, carry):
            for u in range(GROUP):
                s = ch * step + g * GROUP + u
                x = vec_ref[jnp.minimum(index[s], limit - 1)]
                prod[pl.ds(s * wide, vecs), :] = mul(x, tbuf[s], dims)
            return carry

        lax.fori_loop(0, step // GROUP, body, 0)

    plain = (((1,), (0,)), ((), ()))
    across = (((1,), (1,)), ((), ()))

    def gather_sums(index_v, rows, target):
        pick = lax.broadcasted_iota(jnp.int32, (rows, slots), 0) == index_v[...]
        pick = jnp.where(pick, 1.0, 0.0).astype(BF16)

        def body(k, carry):
            high, low = split(prod[pl.ds(k, slots, stride=wide), :])
            target[pl.ds(k, rows, stride=wide), :] = mul(pick, high) + mul(pick, low)
            return carry

        lax.fori_loop(0, vecs, body, 0)

    for y in y_src:
        landed(rv_at(y), left_sem.at[y])
    for ch in range(chunks):
        tile_copy(ch).wait()
        images(ch, rv, row_s, block_rows, plain)
        if ch == chunks // 2:
            relay_z()
    relay_x()
    gather_sums(col_v, block_cols, zp)

    z_order = list(zip(z_far, range(1, outer))) + [(o, 0)]
    x_order = list(zip(x_far, range(1, inner))) + [(i, 0)]
    for z, _ in z_order:
        for x, _ in x_order:
            at = pl.ds(row_of(z, x, 1 - core) * part, part)
            slot = z * inner + x
            send(zp.at[at], zc.at[slot], zc_sem.at[slot], partner)
    take_core()
    for ch in range(chunks // 2):
        images(ch, cv, col_s, block_cols, across)
    for z, _ in z_order:
        for x, dx in x_order:
            slot = z * inner + x
            landed(zc.at[slot], zc_sem.at[slot])
            at = pl.ds(row_of(z, x, core) * part, part)
            zs[slot] = zp[at] + zc[slot]
            if dx:
                send(zs.at[slot], zx.at[dx - 1, z], zx_sem.at[dx - 1, z], (row_of(o, x, core), c))
    for ch in range(chunks // 2, chunks):
        images(ch, cv, col_s, block_cols, across)
    gather_sums(row_v, block_rows, yp)
    for y in y_far:
        dy = (y - c + n_c) % n_c
        send(yp.at[pl.ds(y * part, part)], yl.at[dy], y_sem.at[dy], (r, y))

    def gram_step(a, total):
        at = pl.ds(a * wide, vecs)
        high, low = split(yp[at, :])
        mine = rv[a]
        return total + mul(mine, high, across) + mul(mine, low, across)

    gram = lax.fori_loop(0, block_rows, gram_step, jnp.zeros((vecs, vecs), F32))
    used = 0

    def spread(value, buf, me, far, src, peer):
        nonlocal used
        buf[me] = value
        for f in far:
            send(buf.at[me], buf.at[me], g_sem.at[used + me], peer(f))
        for s in src:
            landed(buf.at[s], g_sem.at[used + s])
        used += buf.shape[0]
        total = buf[0]
        for q in range(1, buf.shape[0]):
            total = total + buf[q]
        return total

    gram = spread(gram, gc, core, [1 - core], [1 - core], lambda f: (row_of(o, i, f), c))
    gram = spread(gram, gx, i, x_far, x_src, lambda f: (row_of(o, f, core), c))

    for z, dz in z_order:
        slot = z * inner + i
        total = zs[slot]
        for d in range(1, inner):
            landed(zx.at[d - 1, z], zx_sem.at[d - 1, z])
            total = total + zx[d - 1, z]
        zs[slot] = total
        if dz:
            send(zs.at[slot], zz.at[dz - 1], zz_sem.at[dz - 1], (row_of(z, i, core), c))

    gram = spread(gram, gy, c, y_far, y_src, lambda f: (r, f))
    gram = spread(gram, gz, o, z_far, z_src, lambda f: (row_of(f, i, core), c))
    gram = gram * (block_cols * n_c * side) ** (-0.5)
    out_g[...] = gram
    y_total = yp[pl.ds(c * part, part), :]
    for d in range(1, n_c):
        landed(yl.at[d], y_sem.at[d])
        y_total = y_total + yl[d]
    out_y[...] = y_total
    z_total = zs[o * inner + i]
    for d in range(1, outer):
        landed(zz.at[d - 1], zz_sem.at[d - 1])
        z_total = z_total + zz[d - 1]
    out_z[...] = z_total
    for copy in sent:
        copy.wait_send()


def finish(y_ref, z_ref, gram_ref, right, left, out_r, out_l, out_g):
    piece, vecs, _ = right.shape
    wide = y_ref.shape[0] // piece
    gram = gram_ref[...]
    out_g[...] = gram
    high, low = split(gram)
    turned_high, turned_low = split(gram.T)
    for t in range(piece):
        at = slice(t * wide, t * wide + vecs)
        out_r[t] = y_ref[at] - (mul(turned_high, right[t]) + mul(turned_low, right[t]))
        out_l[t] = z_ref[at] - (mul(high, left[t]) + mul(low, left[t]))


def solution(mesh):
    n_r, n_c = mesh.shape["row"], mesh.shape["col"]
    half = n_r // 2
    inner = 1 << ((half.bit_length() - 1) // 2)
    outer = half // inner

    def per_device(tiles, tile_row, tile_col, right_vecs, left_vecs):
        slots, side = tiles.shape[2], tiles.shape[3]
        piece, vecs, _ = right_vecs.shape
        chunks = 8
        wide = vecs + PAD
        part = piece * wide
        block_rows, block_cols = piece * n_c, piece * n_r
        planes = outer * inner
        sends = (
            2 * (n_c - 1)
            + (outer - 1)
            + (inner - 1)
            + 1
            + (outer - 1) * inner
            + outer * (inner - 1)
            + planes
            + outer * (inner - 1)
            + (outer - 1)
            + 1
            + (inner - 1)
            + (n_c - 1)
            + (outer - 1)
        )
        vmem = pl.BlockSpec(memory_space=pltpu.VMEM)
        smem = pl.BlockSpec(memory_space=pltpu.SMEM)
        dma = pltpu.SemaphoreType.DMA
        row_s = tile_row.reshape(slots)
        col_s = tile_col.reshape(slots)
        y_total, z_total, gram = pl.pallas_call(
            functools.partial(kernel, (n_r, n_c, outer, inner, chunks)),
            out_shape=(
                jax.ShapeDtypeStruct((part, side), F32),
                jax.ShapeDtypeStruct((part, side), F32),
                jax.ShapeDtypeStruct((vecs, vecs), F32),
            ),
            in_specs=[smem, smem, vmem, vmem, vmem, vmem, pl.BlockSpec(memory_space=pl.ANY)],
            out_specs=(vmem, vmem, vmem),
            scratch_shapes=[
                pltpu.VMEM((slots, side, side), BF16),
                pltpu.VMEM((block_cols, vecs, side), BF16),
                pltpu.VMEM((block_rows, vecs, side), BF16),
                pltpu.VMEM((slots * wide, side), F32),
                pltpu.VMEM((block_cols * wide, side), F32),
                pltpu.VMEM((planes, part, side), F32),
                pltpu.VMEM((planes, part, side), F32),
                pltpu.VMEM((max(inner - 1, 1), outer, part, side), F32),
                pltpu.VMEM((max(outer - 1, 1), part, side), F32),
                pltpu.VMEM((block_rows * wide, side), F32),
                pltpu.VMEM((n_c, part, side), F32),
                pltpu.VMEM((outer, vecs, vecs), F32),
                pltpu.VMEM((inner, vecs, vecs), F32),
                pltpu.VMEM((2, vecs, vecs), F32),
                pltpu.VMEM((n_c, vecs, vecs), F32),
                dma((chunks,)),
                dma((sends,)),
                dma((n_c,)),
                dma((n_r,)),
                dma((planes,)),
                dma((max(inner - 1, 1), outer)),
                dma((max(outer - 1, 1),)),
                dma((n_c,)),
                dma((outer + inner + 2 + n_c,)),
            ],
            compiler_params=pltpu.CompilerParams(
                collective_id=0, has_side_effects=True, vmem_limit_bytes=60 * 1024 * 1024
            ),
            name="arnoldi_step",
        )(row_s, col_s, row_s.reshape(1, slots), col_s.reshape(1, slots), right_vecs, left_vecs, tiles)
        return pl.pallas_call(
            finish,
            out_shape=(
                jax.ShapeDtypeStruct((piece, vecs, side), F32),
                jax.ShapeDtypeStruct((piece, vecs, side), F32),
                jax.ShapeDtypeStruct((vecs, vecs), F32),
            ),
            in_specs=[vmem] * 5,
            out_specs=(vmem, vmem, vmem),
            name="finish",
        )(y_total, z_total, gram, right_vecs, left_vecs)

    placed = (
        P("row", "col", None, None, None),
        P("row", "col", None),
        P("row", "col", None),
        P(("row", "col"), None, None),
        P(("row", "col"), None, None),
    )
    return jax.shard_map(
        per_device,
        mesh=mesh,
        in_specs=placed,
        out_specs=(P(("row", "col"), None, None), P(("row", "col"), None, None), P()),
        check_vma=False,
    )
```

```python
import functools

import jax
import jax.numpy as jnp
from jax import lax
from jax.experimental import pallas as pl
from jax.experimental.pallas import tpu as pltpu
from jax.sharding import PartitionSpec as P

MESH = pl.DeviceIdType.MESH
F32 = jnp.float32
BF16 = jnp.bfloat16
GROUP = 32
PAIR = 2
KGROUP = 8
TOP = 32767.0
LEAST = 2.0**-110
PAD = 1


def split(value):
    high = value.astype(BF16)
    low = (value - high.astype(F32)).astype(BF16)
    return high, low


def mul(a, b, dims=(((1,), (0,)), ((), ()))):
    return lax.dot_general(a, b, dims, preferred_element_type=F32)


def kernel(
    sizes,
    row_s,
    col_s,
    row_v,
    col_v,
    right,
    left,
    tiles,
    out_y,
    out_z,
    out_g,
    tbuf,
    cv,
    rv,
    prod,
    zp,
    zc,
    zs,
    qx_out,
    sx_out,
    qx,
    sx,
    qz_out,
    sz_out,
    qz,
    sz,
    yp,
    yl,
    gz,
    gx,
    gc,
    gy,
    tile_sem,
    send_sem,
    left_sem,
    right_sem,
    zc_sem,
    zx_sem,
    zz_sem,
    sx_sem,
    sz_sem,
    y_sem,
    g_sem,
):
    n_r, n_c, outer, inner, chunks = sizes
    piece, vecs, side = right.shape
    slots = tbuf.shape[0]
    step = slots // chunks
    block_rows = piece * n_c
    block_cols = piece * n_r
    wide = vecs + PAD
    part = piece * wide
    r = lax.axis_index("row")
    c = lax.axis_index("col")
    core = r % 2
    i = (r // 2) % inner
    o = r // (2 * inner)

    def row_of(oo, ii, cc):
        return (oo * inner + ii) * 2 + cc

    partner = (row_of(o, i, 1 - core), c)
    z_far = [(o + d) % outer for d in range(1, outer)]
    z_src = [(o - d + outer) % outer for d in range(1, outer)]
    x_far = [(i + d) % inner for d in range(1, inner)]
    x_src = [(i - d + inner) % inner for d in range(1, inner)]
    y_far = [(c + d) % n_c for d in range(1, n_c)]
    y_src = [(c - d + n_c) % n_c for d in range(1, n_c)]

    def tile_copy(ch):
        at = pl.ds(ch * step, step)
        return pltpu.make_async_copy(tiles.at[0, 0, at], tbuf.at[at], tile_sem.at[ch])

    for ch in range(chunks):
        tile_copy(ch).start()

    barrier = pltpu.get_barrier_semaphore()
    peers = (
        [(row_of(z, i, core), c) for z in z_far]
        + [(row_of(o, x, core), c) for x in x_far]
        + [partner]
        + [(r, y) for y in y_far]
    )
    for peer in peers:
        pl.semaphore_signal(barrier, inc=1, device_id=peer, device_id_type=MESH)
    pl.semaphore_wait(barrier, len(peers))

    sent = []

    def send(src, dst, sem, peer):
        copy = pltpu.make_async_remote_copy(
            src_ref=src,
            dst_ref=dst,
            send_sem=send_sem.at[len(sent)],
            recv_sem=sem,
            device_id=peer,
            device_id_type=MESH,
        )
        copy.start()
        sent.append(copy)

    def landed(ref, sem):
        pltpu.make_async_remote_copy(
            src_ref=ref,
            dst_ref=ref,
            send_sem=send_sem.at[0],
            recv_sem=sem,
            device_id=partner,
            device_id_type=MESH,
        ).wait_recv()

    def cv_at(rr):
        return cv.at[pl.ds(rr * piece, piece)]

    def rv_at(cc):
        return rv.at[pl.ds(cc * piece, piece)]

    for y in y_far:
        send(left, rv_at(c), left_sem.at[c], (r, y))
    for z in z_far:
        send(right, cv_at(r), right_sem.at[r], (row_of(z, i, core), c))
    for x in x_far:
        send(right, cv_at(r), right_sem.at[r], (row_of(o, x, core), c))
    send(right, cv_at(r), right_sem.at[r], partner)
    cv[pl.ds(r * piece, piece)] = right[...]
    rv[pl.ds(c * piece, piece)] = left[...]

    def relay_z():
        for z in z_src:
            got = row_of(z, i, core)
            landed(cv_at(got), right_sem.at[got])
            for x in x_far:
                send(cv_at(got), cv_at(got), right_sem.at[got], (row_of(o, x, core), c))
            send(cv_at(got), cv_at(got), right_sem.at[got], partner)

    def relay_x():
        for z in [o] + z_src:
            for x in x_src:
                got = row_of(z, x, core)
                landed(cv_at(got), right_sem.at[got])
                send(cv_at(got), cv_at(got), right_sem.at[got], partner)

    def take_core():
        for z in [o] + z_src:
            for x in [i] + x_src:
                got = row_of(z, x, 1 - core)
                landed(cv_at(got), right_sem.at[got])

    def images(ch, vec_ref, index, limit, turned):
        def body(g, carry):
            for u in range(0, GROUP, PAIR):
                s = ch * step + g * GROUP + u
                xs = [vec_ref[jnp.minimum(index[s + q], limit - 1)] for q in range(PAIR)]
                ts = [tbuf[s + q] for q in range(PAIR)]
                dims = across if turned else plain
                got = mul(jnp.concatenate(xs, 0), jnp.concatenate(ts, 0 if turned else 1), dims)
                for q in range(PAIR):
                    block = got[q * vecs : (q + 1) * vecs, q * side : (q + 1) * side]
                    prod[pl.ds((s + q) * wide, vecs), :] = block
            return carry

        lax.fori_loop(0, step // GROUP, body, 0)

    plain = (((1,), (0,)), ((), ()))
    across = (((1,), (1,)), ((), ()))

    def gather_sums(index_v, rows, target):
        pick = lax.broadcasted_iota(jnp.int32, (rows, slots), 0) == index_v[...]
        pick = jnp.where(pick, 1.0, 0.0).astype(BF16)
        pick = jnp.concatenate([pick, pick], 1)

        def body(g, carry):
            for u in range(0, KGROUP, PAIR):
                k = g * KGROUP + u
                terms = [split(prod[pl.ds(k + q, slots, stride=wide), :]) for q in range(PAIR)]
                high = jnp.concatenate([t[0] for t in terms], 1)
                low = jnp.concatenate([t[1] for t in terms], 1)
                got = mul(pick, jnp.concatenate([high, low], 0))
                for q in range(PAIR):
                    block = got[:, q * side : (q + 1) * side]
                    target[pl.ds(k + q, rows, stride=wide), :] = block
            return carry

        lax.fori_loop(0, vecs // KGROUP, body, 0)

    for y in y_src:
        landed(rv_at(y), left_sem.at[y])
    for ch in range(chunks):
        tile_copy(ch).wait()
        images(ch, rv, row_s, block_rows, False)
    relay_z()
    gather_sums(col_v, block_cols, zp)

    z_order = list(zip(z_far, range(1, outer))) + [(o, 0)]
    x_order = list(zip(x_far, range(1, inner))) + [(i, 0)]
    for z, _ in z_order:
        for x, _ in x_order:
            at = pl.ds(row_of(z, x, 1 - core) * part, part)
            slot = z * inner + x
            send(zp.at[at], zc.at[slot], zc_sem.at[slot], partner)
    relay_x()
    take_core()
    for ch in range(chunks // 2):
        images(ch, cv, col_s, block_cols, True)
    def encode(block_of, q_ref, s_ref):
        scales = []
        for t in range(piece):
            block = block_of(t)
            top = jnp.maximum(jnp.max(jnp.abs(block), axis=0, keepdims=True), LEAST)
            q_ref[t * vecs : (t + 1) * vecs] = (
                jnp.round(block * (TOP / top)).astype(jnp.int32).astype(jnp.int16)
            )
            scales.append(top * (1.0 / TOP))
        s_ref[...] = jnp.concatenate(scales, 0)

    def decode(q_ref, s_ref, t):
        code = q_ref[t * vecs : (t + 1) * vecs].astype(jnp.int32).astype(F32)
        return code * s_ref[t : t + 1]

    def pair_sum(z, x, t):
        mine = zp[pl.ds(row_of(z, x, core) * part + t * wide, vecs), :]
        return mine + zc[z * inner + x, t * wide : t * wide + vecs]

    for z, _ in z_order:
        for x, dx in x_order:
            slot = z * inner + x
            landed(zc.at[slot], zc_sem.at[slot])
            if dx:
                encode(functools.partial(pair_sum, z, x), qx_out.at[dx - 1, z], sx_out.at[dx - 1, z])
                peer = (row_of(o, x, core), c)
                send(qx_out.at[dx - 1, z], qx.at[dx - 1, z], zx_sem.at[dx - 1, z], peer)
                send(sx_out.at[dx - 1, z], sx.at[dx - 1, z], sx_sem.at[dx - 1, z], peer)
    for ch in range(chunks // 2, chunks):
        images(ch, cv, col_s, block_cols, True)
    gather_sums(row_v, block_rows, yp)
    for y in y_far:
        dy = (y - c + n_c) % n_c
        send(yp.at[pl.ds(y * part, part)], yl.at[dy], y_sem.at[dy], (r, y))

    def gram_step(a, total):
        at = pl.ds(a * wide, vecs)
        high, low = split(yp[at, :])
        mine = rv[a]
        return total + mul(mine, high, across) + mul(mine, low, across)

    gram = lax.fori_loop(0, block_rows, gram_step, jnp.zeros((vecs, vecs), F32))
    used = 0

    def spread(value, buf, me, far, src, peer):
        nonlocal used
        buf[me] = value
        for f in far:
            send(buf.at[me], buf.at[me], g_sem.at[used + me], peer(f))
        for s in src:
            landed(buf.at[s], g_sem.at[used + s])
        used += buf.shape[0]
        total = buf[0]
        for q in range(1, buf.shape[0]):
            total = total + buf[q]
        return total

    gram = spread(gram, gc, core, [1 - core], [1 - core], lambda f: (row_of(o, i, f), c))
    gram = spread(gram, gx, i, x_far, x_src, lambda f: (row_of(o, f, core), c))

    def plane_sum(z, t):
        total = pair_sum(z, i, t)
        for d in range(1, inner):
            total = total + decode(qx.at[d - 1, z], sx.at[d - 1, z], t)
        return total

    for z, dz in z_order:
        for d in range(1, inner):
            landed(qx.at[d - 1, z], zx_sem.at[d - 1, z])
            landed(sx.at[d - 1, z], sx_sem.at[d - 1, z])
        if dz:
            encode(functools.partial(plane_sum, z), qz_out.at[dz - 1], sz_out.at[dz - 1])
            peer = (row_of(z, i, core), c)
            send(qz_out.at[dz - 1], qz.at[dz - 1], zz_sem.at[dz - 1], peer)
            send(sz_out.at[dz - 1], sz.at[dz - 1], sz_sem.at[dz - 1], peer)
        else:
            for t in range(piece):
                zs[t * vecs : (t + 1) * vecs] = plane_sum(z, t)

    gram = spread(gram, gy, c, y_far, y_src, lambda f: (r, f))
    gram = spread(gram, gz, o, z_far, z_src, lambda f: (row_of(f, i, core), c))
    gram = gram * (block_cols * n_c * side) ** (-0.5)
    out_g[...] = gram
    y_total = yp[pl.ds(c * part, part), :]
    for d in range(1, n_c):
        landed(yl.at[d], y_sem.at[d])
        y_total = y_total + yl[d]
    out_y[...] = y_total
    for d in range(1, outer):
        landed(qz.at[d - 1], zz_sem.at[d - 1])
        landed(sz.at[d - 1], sz_sem.at[d - 1])
    for t in range(piece):
        total = zs[t * vecs : (t + 1) * vecs]
        for d in range(1, outer):
            total = total + decode(qz.at[d - 1], sz.at[d - 1], t)
        out_z[t] = total
    for copy in sent:
        copy.wait_send()


def finish(y_ref, z_ref, gram_ref, right, left, out_r, out_l, out_g):
    piece, vecs, _ = right.shape
    wide = y_ref.shape[0] // piece
    gram = gram_ref[...]
    out_g[...] = gram
    high, low = split(gram)
    turned_high, turned_low = split(gram.T)
    for t in range(piece):
        at = slice(t * wide, t * wide + vecs)
        out_r[t] = y_ref[at] - (mul(turned_high, right[t]) + mul(turned_low, right[t]))
        out_l[t] = z_ref[t] - (mul(high, left[t]) + mul(low, left[t]))


def solution(mesh):
    n_r, n_c = mesh.shape["row"], mesh.shape["col"]
    half = n_r // 2
    inner = 1 << ((half.bit_length() - 1) // 2)
    outer = half // inner

    def per_device(tiles, tile_row, tile_col, right_vecs, left_vecs):
        slots, side = tiles.shape[2], tiles.shape[3]
        piece, vecs, _ = right_vecs.shape
        chunks = 8
        wide = vecs + PAD
        part = piece * wide
        block_rows, block_cols = piece * n_c, piece * n_r
        planes = outer * inner
        near, far = max(inner - 1, 1), max(outer - 1, 1)
        sends = (
            2 * (n_c - 1)
            + (outer - 1)
            + (inner - 1)
            + 1
            + (outer - 1) * inner
            + outer * (inner - 1)
            + planes
            + 2 * outer * (inner - 1)
            + 2 * (outer - 1)
            + 1
            + (inner - 1)
            + (n_c - 1)
            + (outer - 1)
        )
        vmem = pl.BlockSpec(memory_space=pltpu.VMEM)
        smem = pl.BlockSpec(memory_space=pltpu.SMEM)
        dma = pltpu.SemaphoreType.DMA
        row_s = tile_row.reshape(slots)
        col_s = tile_col.reshape(slots)
        y_total, z_total, gram = pl.pallas_call(
            functools.partial(kernel, (n_r, n_c, outer, inner, chunks)),
            out_shape=(
                jax.ShapeDtypeStruct((part, side), F32),
                jax.ShapeDtypeStruct((piece, vecs, side), F32),
                jax.ShapeDtypeStruct((vecs, vecs), F32),
            ),
            in_specs=[smem, smem, vmem, vmem, vmem, vmem, pl.BlockSpec(memory_space=pl.ANY)],
            out_specs=(vmem, vmem, vmem),
            scratch_shapes=[
                pltpu.VMEM((slots, side, side), BF16),
                pltpu.VMEM((block_cols, vecs, side), BF16),
                pltpu.VMEM((block_rows, vecs, side), BF16),
                pltpu.VMEM((slots * wide, side), F32),
                pltpu.VMEM((block_cols * wide, side), F32),
                pltpu.VMEM((planes, part, side), F32),
                pltpu.VMEM((piece * vecs, side), F32),
                *[
                    pltpu.VMEM(lead + shape, kind)
                    for lead in [(near, outer)] * 2 + [(far,)] * 2
                    for shape, kind in [((piece * vecs, side), jnp.int16), ((piece, side), F32)]
                ],
                pltpu.VMEM((block_rows * wide, side), F32),
                pltpu.VMEM((n_c, part, side), F32),
                pltpu.VMEM((outer, vecs, vecs), F32),
                pltpu.VMEM((inner, vecs, vecs), F32),
                pltpu.VMEM((2, vecs, vecs), F32),
                pltpu.VMEM((n_c, vecs, vecs), F32),
                dma((chunks,)),
                dma((sends,)),
                dma((n_c,)),
                dma((n_r,)),
                dma((planes,)),
                *[dma((near, outer)), dma((far,))] * 2,
                dma((n_c,)),
                dma((outer + inner + 2 + n_c,)),
            ],
            compiler_params=pltpu.CompilerParams(
                collective_id=0, has_side_effects=True, vmem_limit_bytes=60 * 1024 * 1024
            ),
            name="arnoldi_step",
        )(row_s, col_s, row_s.reshape(1, slots), col_s.reshape(1, slots), right_vecs, left_vecs, tiles)
        return pl.pallas_call(
            finish,
            out_shape=(
                jax.ShapeDtypeStruct((piece, vecs, side), F32),
                jax.ShapeDtypeStruct((piece, vecs, side), F32),
                jax.ShapeDtypeStruct((vecs, vecs), F32),
            ),
            in_specs=[vmem] * 5,
            out_specs=(vmem, vmem, vmem),
            name="finish",
        )(y_total, z_total, gram, right_vecs, left_vecs)

    placed = (
        P("row", "col", None, None, None),
        P("row", "col", None),
        P("row", "col", None),
        P(("row", "col"), None, None),
        P(("row", "col"), None, None),
    )
    return jax.shard_map(
        per_device,
        mesh=mesh,
        in_specs=placed,
        out_specs=(P(("row", "col"), None, None), P(("row", "col"), None, None), P()),
        check_vma=False,
    )
```

```python
import functools

import jax
import jax.numpy as jnp
from jax import lax
from jax.experimental import pallas as pl
from jax.experimental.pallas import tpu as pltpu
from jax.sharding import PartitionSpec as P

MESH = pl.DeviceIdType.MESH
F32 = jnp.float32
BF16 = jnp.bfloat16
GROUP = 32
PAIR = 2
KGROUP = 8
TOP = 32767.0
LEAST = 2.0**-110
PAD = 1


def split(value):
    high = value.astype(BF16)
    low = (value - high.astype(F32)).astype(BF16)
    return high, low


def mul(a, b, dims=(((1,), (0,)), ((), ()))):
    return lax.dot_general(a, b, dims, preferred_element_type=F32)


def kernel(
    sizes,
    row_s,
    col_s,
    row_v,
    col_v,
    right,
    left,
    tiles,
    out_y,
    out_z,
    out_g,
    tbuf,
    cv,
    rv,
    prod,
    zp,
    zc,
    zs,
    qx_out,
    sx_out,
    qx,
    sx,
    qz_out,
    sz_out,
    qz,
    sz,
    yp,
    yl,
    ga,
    gb,
    tile_sem,
    send_sem,
    left_sem,
    right_sem,
    zc_sem,
    zx_sem,
    zz_sem,
    sx_sem,
    sz_sem,
    y_sem,
    g_sem,
):
    n_r, n_c, outer, inner, chunks = sizes
    piece, vecs, side = right.shape
    slots = tbuf.shape[0]
    step = slots // chunks
    block_rows = piece * n_c
    block_cols = piece * n_r
    wide = vecs + PAD
    part = piece * wide
    r = lax.axis_index("row")
    c = lax.axis_index("col")
    core = r % 2
    i = (r // 2) % inner
    o = r // (2 * inner)

    def row_of(oo, ii, cc):
        return (oo * inner + ii) * 2 + cc

    partner = (row_of(o, i, 1 - core), c)
    z_far = [(o + d) % outer for d in range(1, outer)]
    z_src = [(o - d + outer) % outer for d in range(1, outer)]
    x_far = [(i + d) % inner for d in range(1, inner)]
    x_src = [(i - d + inner) % inner for d in range(1, inner)]
    y_far = [(c + d) % n_c for d in range(1, n_c)]
    y_src = [(c - d + n_c) % n_c for d in range(1, n_c)]

    def tile_copy(ch):
        at = pl.ds(ch * step, step)
        return pltpu.make_async_copy(tiles.at[0, 0, at], tbuf.at[at], tile_sem.at[ch])

    for ch in range(chunks):
        tile_copy(ch).start()

    barrier = pltpu.get_barrier_semaphore()
    near = [
        ((i + d) % inner, (core + e) % 2, (i - d + inner) % inner)
        for d in range(inner)
        for e in range(2)
        if d or e
    ]
    wide_set = [
        ((o + d) % outer, (c + e) % n_c, (o - d + outer) % outer, (c - e + n_c) % n_c)
        for d in range(outer)
        for e in range(n_c)
        if d or e
    ]
    near_peers = [(row_of(o, x, cc), c) for x, cc, _ in near]
    near_src = [x * 2 + cc for _, cc, x in near]
    wide_peers = [(row_of(z, i, core), y) for z, y, _, _ in wide_set]
    wide_src = [z * n_c + y for _, _, z, y in wide_set]
    peers = near_peers + wide_peers
    for peer in peers:
        pl.semaphore_signal(barrier, inc=1, device_id=peer, device_id_type=MESH)
    pl.semaphore_wait(barrier, len(peers))

    sent = []

    def send(src, dst, sem, peer):
        copy = pltpu.make_async_remote_copy(
            src_ref=src,
            dst_ref=dst,
            send_sem=send_sem.at[len(sent)],
            recv_sem=sem,
            device_id=peer,
            device_id_type=MESH,
        )
        copy.start()
        sent.append(copy)

    def landed(ref, sem):
        pltpu.make_async_remote_copy(
            src_ref=ref,
            dst_ref=ref,
            send_sem=send_sem.at[0],
            recv_sem=sem,
            device_id=partner,
            device_id_type=MESH,
        ).wait_recv()

    def cv_at(rr):
        return cv.at[pl.ds(rr * piece, piece)]

    def rv_at(cc):
        return rv.at[pl.ds(cc * piece, piece)]

    for y in y_far:
        send(left, rv_at(c), left_sem.at[c], (r, y))
    for z in z_far:
        send(right, cv_at(r), right_sem.at[r], (row_of(z, i, core), c))
    for x in x_far:
        send(right, cv_at(r), right_sem.at[r], (row_of(o, x, core), c))
    send(right, cv_at(r), right_sem.at[r], partner)
    cv[pl.ds(r * piece, piece)] = right[...]
    rv[pl.ds(c * piece, piece)] = left[...]

    def relay_z():
        for z in z_src:
            got = row_of(z, i, core)
            landed(cv_at(got), right_sem.at[got])
            for x in x_far:
                send(cv_at(got), cv_at(got), right_sem.at[got], (row_of(o, x, core), c))
            send(cv_at(got), cv_at(got), right_sem.at[got], partner)

    def relay_x():
        for z in [o] + z_src:
            for x in x_src:
                got = row_of(z, x, core)
                landed(cv_at(got), right_sem.at[got])
                send(cv_at(got), cv_at(got), right_sem.at[got], partner)

    def take_core():
        for z in [o] + z_src:
            for x in [i] + x_src:
                got = row_of(z, x, 1 - core)
                landed(cv_at(got), right_sem.at[got])

    def images(ch, vec_ref, index, limit, turned):
        def body(g, carry):
            for u in range(0, GROUP, PAIR):
                s = ch * step + g * GROUP + u
                xs = [vec_ref[jnp.minimum(index[s + q], limit - 1)] for q in range(PAIR)]
                ts = [tbuf[s + q] for q in range(PAIR)]
                dims = across if turned else plain
                got = mul(jnp.concatenate(xs, 0), jnp.concatenate(ts, 0 if turned else 1), dims)
                for q in range(PAIR):
                    block = got[q * vecs : (q + 1) * vecs, q * side : (q + 1) * side]
                    prod[pl.ds((s + q) * wide, vecs), :] = block
            return carry

        lax.fori_loop(0, step // GROUP, body, 0)

    plain = (((1,), (0,)), ((), ()))
    across = (((1,), (1,)), ((), ()))

    def gather_sums(index_v, rows, target):
        pick = lax.broadcasted_iota(jnp.int32, (rows, slots), 0) == index_v[...]
        pick = jnp.where(pick, 1.0, 0.0).astype(BF16)
        pick = jnp.concatenate([pick, pick], 1)

        def body(g, carry):
            for u in range(0, KGROUP, PAIR):
                k = g * KGROUP + u
                terms = [split(prod[pl.ds(k + q, slots, stride=wide), :]) for q in range(PAIR)]
                high = jnp.concatenate([t[0] for t in terms], 1)
                low = jnp.concatenate([t[1] for t in terms], 1)
                got = mul(pick, jnp.concatenate([high, low], 0))
                for q in range(PAIR):
                    block = got[:, q * side : (q + 1) * side]
                    target[pl.ds(k + q, rows, stride=wide), :] = block
            return carry

        lax.fori_loop(0, vecs // KGROUP, body, 0)

    for y in y_src:
        landed(rv_at(y), left_sem.at[y])
    for ch in range(chunks):
        tile_copy(ch).wait()
        images(ch, rv, row_s, block_rows, False)
    relay_z()
    gather_sums(col_v, block_cols, zp)

    z_order = list(zip(z_far, range(1, outer))) + [(o, 0)]
    x_order = list(zip(x_far, range(1, inner))) + [(i, 0)]
    for z, _ in z_order:
        for x, _ in x_order:
            at = pl.ds(row_of(z, x, 1 - core) * part, part)
            slot = z * inner + x
            send(zp.at[at], zc.at[slot], zc_sem.at[slot], partner)
    relay_x()
    take_core()

    def gram_step(p, total):
        sums, mates = [], []
        for t in range(piece):
            high, low = split(zp[pl.ds(p * part + t * wide, vecs), :])
            sums.append(jnp.concatenate([high, low], 0))
            mates.append(cv[p * piece + t])
        return total + mul(jnp.concatenate(sums, 1), jnp.concatenate(mates, 1), across)

    total = lax.fori_loop(0, n_r, gram_step, jnp.zeros((2 * vecs, vecs), F32))

    def spread(value, buf, base, me, far):
        buf[me] = value
        for peer in far:
            send(buf.at[me], buf.at[me], g_sem.at[base + me], peer)

    def collect(buf, base, src):
        for q in src:
            landed(buf.at[q], g_sem.at[base + q])
        total = buf[0]
        for q in range(1, buf.shape[0]):
            total = total + buf[q]
        return total

    spread(total[:vecs] + total[vecs:], ga, 0, i * 2 + core, near_peers)
    def encode(block_of, q_ref, s_ref):
        scales = []
        for t in range(piece):
            block = block_of(t)
            top = jnp.maximum(jnp.max(jnp.abs(block), axis=0, keepdims=True), LEAST)
            q_ref[t * vecs : (t + 1) * vecs] = (
                jnp.round(block * (TOP / top)).astype(jnp.int32).astype(jnp.int16)
            )
            scales.append(top * (1.0 / TOP))
        s_ref[...] = jnp.concatenate(scales, 0)

    def decode(q_ref, s_ref, t):
        code = q_ref[t * vecs : (t + 1) * vecs].astype(jnp.int32).astype(F32)
        return code * s_ref[t : t + 1]

    def pair_sum(z, x, t):
        mine = zp[pl.ds(row_of(z, x, core) * part + t * wide, vecs), :]
        return mine + zc[z * inner + x, t * wide : t * wide + vecs]

    for z, _ in z_order:
        for x, dx in x_order:
            slot = z * inner + x
            landed(zc.at[slot], zc_sem.at[slot])
            if dx:
                encode(functools.partial(pair_sum, z, x), qx_out.at[dx - 1, z], sx_out.at[dx - 1, z])
                peer = (row_of(o, x, core), c)
                send(qx_out.at[dx - 1, z], qx.at[dx - 1, z], zx_sem.at[dx - 1, z], peer)
                send(sx_out.at[dx - 1, z], sx.at[dx - 1, z], sx_sem.at[dx - 1, z], peer)
    for ch in range(chunks // 2):
        images(ch, cv, col_s, block_cols, True)
    spread(collect(ga, 0, near_src), gb, 2 * inner, o * n_c + c, wide_peers)
    for ch in range(chunks // 2, chunks):
        images(ch, cv, col_s, block_cols, True)
    gather_sums(row_v, block_rows, yp)
    for y in y_far:
        dy = (y - c + n_c) % n_c
        send(yp.at[pl.ds(y * part, part)], yl.at[dy], y_sem.at[dy], (r, y))

    def plane_sum(z, t):
        total = pair_sum(z, i, t)
        for d in range(1, inner):
            total = total + decode(qx.at[d - 1, z], sx.at[d - 1, z], t)
        return total

    for z, dz in z_order:
        for d in range(1, inner):
            landed(qx.at[d - 1, z], zx_sem.at[d - 1, z])
            landed(sx.at[d - 1, z], sx_sem.at[d - 1, z])
        if dz:
            encode(functools.partial(plane_sum, z), qz_out.at[dz - 1], sz_out.at[dz - 1])
            peer = (row_of(z, i, core), c)
            send(qz_out.at[dz - 1], qz.at[dz - 1], zz_sem.at[dz - 1], peer)
            send(sz_out.at[dz - 1], sz.at[dz - 1], sz_sem.at[dz - 1], peer)
        else:
            for t in range(piece):
                zs[t * vecs : (t + 1) * vecs] = plane_sum(z, t)

    gram = collect(gb, 2 * inner, wide_src)
    gram = gram * (block_cols * n_c * side) ** (-0.5)
    out_g[...] = gram
    y_total = yp[pl.ds(c * part, part), :]
    for d in range(1, n_c):
        landed(yl.at[d], y_sem.at[d])
        y_total = y_total + yl[d]
    out_y[...] = y_total
    for d in range(1, outer):
        landed(qz.at[d - 1], zz_sem.at[d - 1])
        landed(sz.at[d - 1], sz_sem.at[d - 1])
    for t in range(piece):
        total = zs[t * vecs : (t + 1) * vecs]
        for d in range(1, outer):
            total = total + decode(qz.at[d - 1], sz.at[d - 1], t)
        out_z[t] = total
    for copy in sent:
        copy.wait_send()


def finish(y_ref, z_ref, gram_ref, right, left, out_r, out_l, out_g):
    piece, vecs, _ = right.shape
    wide = y_ref.shape[0] // piece
    gram = gram_ref[...]
    out_g[...] = gram
    high, low = split(gram)
    turned_high, turned_low = split(gram.T)
    for t in range(piece):
        at = slice(t * wide, t * wide + vecs)
        out_r[t] = y_ref[at] - (mul(turned_high, right[t]) + mul(turned_low, right[t]))
        out_l[t] = z_ref[t] - (mul(high, left[t]) + mul(low, left[t]))


def solution(mesh):
    n_r, n_c = mesh.shape["row"], mesh.shape["col"]
    half = n_r // 2
    inner = 1 << ((half.bit_length() - 1) // 2)
    outer = half // inner

    def per_device(tiles, tile_row, tile_col, right_vecs, left_vecs):
        slots, side = tiles.shape[2], tiles.shape[3]
        piece, vecs, _ = right_vecs.shape
        chunks = 8
        wide = vecs + PAD
        part = piece * wide
        block_rows, block_cols = piece * n_c, piece * n_r
        planes = outer * inner
        near, far = max(inner - 1, 1), max(outer - 1, 1)
        sends = (
            2 * (n_c - 1)
            + (outer - 1)
            + (inner - 1)
            + 1
            + (outer - 1) * inner
            + outer * (inner - 1)
            + planes
            + 2 * outer * (inner - 1)
            + 2 * (outer - 1)
            + (2 * inner - 1)
            + (outer * n_c - 1)
        )
        vmem = pl.BlockSpec(memory_space=pltpu.VMEM)
        smem = pl.BlockSpec(memory_space=pltpu.SMEM)
        dma = pltpu.SemaphoreType.DMA
        row_s = tile_row.reshape(slots)
        col_s = tile_col.reshape(slots)
        y_total, z_total, gram = pl.pallas_call(
            functools.partial(kernel, (n_r, n_c, outer, inner, chunks)),
            out_shape=(
                jax.ShapeDtypeStruct((part, side), F32),
                jax.ShapeDtypeStruct((piece, vecs, side), F32),
                jax.ShapeDtypeStruct((vecs, vecs), F32),
            ),
            in_specs=[smem, smem, vmem, vmem, vmem, vmem, pl.BlockSpec(memory_space=pl.ANY)],
            out_specs=(vmem, vmem, vmem),
            scratch_shapes=[
                pltpu.VMEM((slots, side, side), BF16),
                pltpu.VMEM((block_cols, vecs, side), BF16),
                pltpu.VMEM((block_rows, vecs, side), BF16),
                pltpu.VMEM((slots * wide, side), F32),
                pltpu.VMEM((block_cols * wide, side), F32),
                pltpu.VMEM((planes, part, side), F32),
                pltpu.VMEM((piece * vecs, side), F32),
                *[
                    pltpu.VMEM(lead + shape, kind)
                    for lead in [(near, outer)] * 2 + [(far,)] * 2
                    for shape, kind in [((piece * vecs, side), jnp.int16), ((piece, side), F32)]
                ],
                pltpu.VMEM((block_rows * wide, side), F32),
                pltpu.VMEM((n_c, part, side), F32),
                pltpu.VMEM((2 * inner, vecs, vecs), F32),
                pltpu.VMEM((outer * n_c, vecs, vecs), F32),
                dma((chunks,)),
                dma((sends,)),
                dma((n_c,)),
                dma((n_r,)),
                dma((planes,)),
                *[dma((near, outer)), dma((far,))] * 2,
                dma((n_c,)),
                dma((2 * inner + outer * n_c,)),
            ],
            compiler_params=pltpu.CompilerParams(
                collective_id=0, has_side_effects=True, vmem_limit_bytes=60 * 1024 * 1024
            ),
            name="arnoldi_step",
        )(row_s, col_s, row_s.reshape(1, slots), col_s.reshape(1, slots), right_vecs, left_vecs, tiles)
        return pl.pallas_call(
            finish,
            out_shape=(
                jax.ShapeDtypeStruct((piece, vecs, side), F32),
                jax.ShapeDtypeStruct((piece, vecs, side), F32),
                jax.ShapeDtypeStruct((vecs, vecs), F32),
            ),
            in_specs=[vmem] * 5,
            out_specs=(vmem, vmem, vmem),
            name="finish",
        )(y_total, z_total, gram, right_vecs, left_vecs)

    placed = (
        P("row", "col", None, None, None),
        P("row", "col", None),
        P("row", "col", None),
        P(("row", "col"), None, None),
        P(("row", "col"), None, None),
    )
    return jax.shard_map(
        per_device,
        mesh=mesh,
        in_specs=placed,
        out_specs=(P(("row", "col"), None, None), P(("row", "col"), None, None), P()),
        check_vma=False,
    )
```
